512 devices in a mesh: ctx: 32 (over z_hi, y, core), tp: 16 (over x, z_lo).
Axes of the slice: x: 4, y: 8, z: 8 (z_hi: 2, z_lo: 4; z = z_hi * 4 + z_lo), core: 2. Of those that a mesh axis runs over, the one named last changes fastest.
Arguments:
- queries: bfloat16 [12288, 4096], P('ctx', 'tp')
- keys: bfloat16 [12288, 4096], P('ctx', 'tp')
- values: bfloat16 [12288, 4096], P('ctx', 'tp')
- out_gate: bfloat16 [12288, 4096], P('ctx', 'tp'), may hold values from -6 to 6
- in_gate: bfloat16 [12288, 4096], P('ctx', 'tp'), may hold values from -6 to 6
- norm_gain: float32 [4096], P('tp'), may hold values from 0.5 to 1.5
- skip_gain: float32 [4096], P('tp'), may hold values from 0.5 to 1.5
- rates: float32 [4096, 16], P('tp'), may hold values from 8.138021e-06 to 0.03
- residues: float32 [4096, 16], P('tp'), may hold values from -1.5 to 1.5
- block_order: int32 [96], replicated, may hold values from 0 to 95, each once
Outputs:
- attn_out: bfloat16 [12288, 4096], P('ctx', 'tp')
- hyena_out: bfloat16 [12288, 4096], P('ctx', 'tp')
The draws below stay inside these ranges and needn't reach their ends.
Inputs may be any that keep to these rules, and one draw needn't show every extreme that they name: `block_order`: a permutation of the 96 sequence blocks: every block appears once.
All inputs are finite; a program needn't handle non-finite values.
Results may differ from the reference program's by a relative error of at most 0.015.
Values may be sent and summed in bfloat16 or wider, within the bound.
A program may use at most 64 MiB of HBM per device.

```python
import math
import jax
import jax.numpy as jnp
from jax import lax

HEADS = 32
HEAD_DIM = 128
MODES = 16
BLK = 128
TOK_DEV = 384
TOKENS = 12288
NBLK = 96
CHAN = 4096


def base_field(key):
    return jnp.clip(jax.random.normal(key, (TOKENS, HEADS, HEAD_DIM), jnp.float32), -6.0, 6.0)


def draw_queries(key, part):
    field = base_field(jax.random.fold_in(key, 1))
    return field.reshape(TOKENS, HEADS * HEAD_DIM).astype(jnp.bfloat16)


def draw_keys(key, part):
    field = base_field(jax.random.fold_in(key, 2))
    return field.reshape(TOKENS, HEADS * HEAD_DIM).astype(jnp.bfloat16)


def draw_values(key, part):
    columns = HEADS * HEAD_DIM
    raw_values = jnp.clip(jax.random.normal(jax.random.fold_in(key, 3), (TOKENS, columns), jnp.float32), -4.0, 4.0)
    column_ids = jnp.arange(columns, dtype=jnp.float32)
    spread_cols = jnp.exp(jax.random.uniform(jax.random.fold_in(key, 4), (columns,), jnp.float32, 0.0, 2.3))
    rising = jnp.exp(1.0986 * column_ids / columns)
    field = raw_values * (spread_cols * rising)[None, :] * 0.3
    return field.astype(jnp.bfloat16)


def steps_of(key, extent, shards, low, largest):
    def one(dim, parts):
        heights = jax.random.uniform(jax.random.fold_in(jax.random.fold_in(key, 6), dim), (parts,), jnp.float32, low / len(shards), largest / len(shards))
        return jnp.repeat(jnp.exp(heights), extent[dim] // parts).reshape((-1,) + (1,) * (len(extent) - dim - 1))

    gain = one(*shards[0])
    for cut in shards[1:]:
        gain = gain * one(*cut)
    return gain


def scatter_about(stream_key, shape, scale, limit, split=(), held_as=jnp.bfloat16):
    values = scale * jax.random.normal(stream_key, shape, jnp.float32)
    if split:
        values = values * steps_of(stream_key, shape, split, -0.22, 0.18)
    return jnp.clip(values, -limit, limit).astype(held_as)


def setup_inputs(seed: int = 0) -> dict:
    splits = jax.random.split(jax.random.key(seed), 11)
    queries = draw_queries(jax.random.fold_in(splits[10], 71), 0)
    keys = draw_keys(jax.random.fold_in(splits[10], 71), 0)
    values = draw_values(jax.random.fold_in(splits[10], 71), 0)
    out_gate = scatter_about(splits[3], (TOKENS, CHAN), 1.0, 6.0, ((0, 32), (1, 16)))
    in_gate = scatter_about(splits[4], (TOKENS, CHAN), 1.0, 6.0, ((0, 32), (1, 16)))
    norm_gain = jnp.clip(1.0 + 0.1 * jax.random.normal(splits[5], (CHAN,), jnp.float32), 0.5, 1.5)
    skip_gain = jnp.clip(0.5 + 1.0 * jax.random.uniform(splits[6], (CHAN,), jnp.float32) ** steps_of(splits[6], (CHAN,), ((0, 16),), -0.2, 0.2), 0.5, 1.5)
    rates = jnp.clip(jnp.exp(math.log(0.03) - 8.2124056 * jax.random.uniform(splits[7], (CHAN, MODES), jnp.float32) ** steps_of(splits[7], (CHAN, MODES), ((0, 16),), -0.2, 0.2)), 8.138021257764194e-06, 0.03)
    residues = scatter_about(splits[8], (CHAN, MODES), MODES ** -0.5, 1.5, ((0, 16),), jnp.float32)
    block_order = jax.random.permutation(splits[9], NBLK).astype(jnp.int32)
    return {"queries": queries, "keys": keys, "values": values, "out_gate": out_gate, "in_gate": in_gate, "norm_gain": norm_gain, "skip_gain": skip_gain, "rates": rates, "residues": residues, "block_order": block_order}


def stored_positions(block_order):
    row_ids = jnp.arange(TOKENS, dtype=jnp.int32)
    return block_order[row_ids // BLK] * BLK + row_ids % BLK

def attend_head(operands):
    query_head, key_head, value_head, positions = operands
    scaling = HEAD_DIM ** (-0.5)

    def one_block(block_index):
        query_block = lax.dynamic_slice_in_dim(query_head, block_index * TOK_DEV, TOK_DEV, 0)
        query_pos = lax.dynamic_slice_in_dim(positions, block_index * TOK_DEV, TOK_DEV, 0)
        scores = jnp.dot(query_block, key_head.T, preferred_element_type=jnp.float32) * scaling
        scores = jnp.where(positions[None, :] <= query_pos[:, None], scores, -jnp.inf)
        row_max = lax.optimization_barrier(jnp.max(scores, axis=1, keepdims=True))
        expo = jnp.exp(scores - row_max)
        totals = lax.optimization_barrier(jnp.sum(expo, axis=1))
        probs = expo.astype(jnp.bfloat16)
        summed = jnp.dot(probs, value_head, preferred_element_type=jnp.float32)
        return summed / totals[:, None]
    block_ids = jnp.arange(TOKENS // TOK_DEV, dtype=jnp.int32)
    return lax.map(one_block, block_ids).reshape(TOKENS, HEAD_DIM)

def conv_group(operands):
    signal, decay_rate, residue = operands
    times_f = jnp.arange(TOKENS, dtype=decay_rate.dtype)
    weight = residue * jnp.sqrt(-jnp.expm1(-2.0 * decay_rate))
    decays = jnp.exp(-decay_rate[:, :, None] * times_f[None, None, :])
    filt = lax.optimization_barrier(jnp.sum(weight[:, :, None] * decays, axis=1))
    length = 2 * TOKENS
    spectrum = jnp.fft.rfft(signal, n=length, axis=1) * jnp.fft.rfft(filt, n=length, axis=1)
    return jnp.fft.irfft(spectrum, n=length, axis=1)[:, :TOKENS]

def reference(queries, keys, values, out_gate, in_gate, norm_gain, skip_gain, rates, residues, block_order):
    positions = stored_positions(block_order)
    query_all = queries.reshape(TOKENS, HEADS, HEAD_DIM).transpose(1, 0, 2)
    key_all = keys.reshape(TOKENS, HEADS, HEAD_DIM).transpose(1, 0, 2)
    value_all = values.reshape(TOKENS, HEADS, HEAD_DIM).transpose(1, 0, 2)
    pos_all = jnp.broadcast_to(positions, (HEADS, TOKENS))
    heads_out = lax.map(attend_head, (query_all, key_all, value_all, pos_all))
    attn_out = heads_out.transpose(1, 0, 2).reshape(TOKENS, HEADS * HEAD_DIM).astype(jnp.bfloat16)
    attn_f = attn_out.astype(jnp.float32)
    mean_square = lax.optimization_barrier(jnp.sum(attn_f * attn_f, axis=1)) / CHAN
    scaled = lax.rsqrt(mean_square + 1e-06)
    mixed = (attn_f * scaled[:, None] * norm_gain[None, :] * in_gate.astype(jnp.float32)).astype(jnp.bfloat16)
    inverse = jnp.zeros((NBLK,), jnp.int32).at[block_order].set(jnp.arange(NBLK, dtype=jnp.int32))
    pos_ids = jnp.arange(TOKENS, dtype=jnp.int32)
    row_of_pos = inverse[pos_ids // BLK] * BLK + pos_ids % BLK
    mixed_pos = mixed.astype(jnp.float32)[row_of_pos]
    grouped = mixed_pos.T.reshape(HEADS, HEAD_DIM, TOKENS)
    rate_groups = rates.reshape(HEADS, HEAD_DIM, MODES)
    residue_groups = residues.reshape(HEADS, HEAD_DIM, MODES)
    conv_pos = lax.map(conv_group, (grouped, rate_groups, residue_groups))
    conv_pos = conv_pos.reshape(CHAN, TOKENS).T
    long_conv = conv_pos[positions].astype(jnp.bfloat16)
    hyena_out = out_gate.astype(jnp.float32) * (long_conv.astype(jnp.float32) + skip_gain[None, :] * mixed.astype(jnp.float32))
    return (attn_out, hyena_out.astype(jnp.bfloat16))
```

```python
import functools
import math

import jax
import jax.numpy as jnp
from jax import lax
from jax.experimental import pallas as pl
from jax.experimental.pallas import tpu as pltpu
from jax.sharding import PartitionSpec as P

HD = 128
BLK = 128
MODES = 16
NB = 3
ROWS = NB * BLK
EXP_SCALE = math.log2(math.e) / math.sqrt(HD)
NEG = -1e30
MESH = pl.DeviceIdType.MESH
F32 = jnp.float32
BF16 = jnp.bfloat16


def body(
    nctx, ntp, bo_ref, row_of_ref,
    q_ref, k_ref, v_ref, og_ref, ig_ref, ng_ref, sg_ref, dec_ref, wgt_ref, blkdec_ref,
    aout_ref, hout_ref,
    kv, qt, zsend_kv, zsend_q, acc, mx, qpos,
    oz_send, oz_recv, ss_send, ss_recv, sq, xs, ys, mixed,
    ends, gath, prefix, reply, enter,
    ring_ss, ring_rs, sib_ss, sib_rs, z_ss, z_rs, tp_ss, tp_rs, e_ss, e_rs, r_ss, r_rs,
):
    ny = nctx // 4
    half = nctx // 2
    per = MODES // half if MODES >= half else 1
    ctx = lax.axis_index("ctx")
    tp = lax.axis_index("tp")
    core = lax.rem(ctx, 2)
    y = lax.rem(ctx // 2, ny)
    zh = ctx // half
    step_dir = 1 - 2 * core

    def at(z, yy, c):
        return z * half + lax.rem(yy + 2 * ny, ny) * 2 + c

    nxt = (at(zh, y + step_dir, core), tp)
    sib = (at(zh, y, 1 - core), tp)
    partner = (lax.rem(ctx + half, nctx), tp)

    barrier = pltpu.get_barrier_semaphore()

    @pl.loop(1, nctx)
    def _(i):
        pl.semaphore_signal(barrier, inc=1, device_id=(lax.rem(ctx + i, nctx), tp), device_id_type=MESH)

    @pl.loop(1, ntp)
    def _(i):
        pl.semaphore_signal(barrier, inc=1, device_id=(ctx, lax.rem(tp + i, ntp)), device_id_type=MESH)

    own_cols = pl.ds(pl.multiple_of(zh * HD, HD), HD)
    oth_cols = pl.ds(pl.multiple_of((1 - zh) * HD, HD), HD)

    def put_kv(dst, cols):
        dst[0:ROWS, :] = k_ref[:, cols]
        for b in range(NB):
            blk = v_ref[b * BLK:(b + 1) * BLK, cols].astype(F32)
            dst[ROWS + b * BLK:ROWS + (b + 1) * BLK, :] = blk.T.astype(BF16)

    put_kv(kv.at[0, 0, 0], own_cols)
    put_kv(zsend_kv, oth_cols)
    qt[0] = q_ref[:, own_cols].astype(F32).T.astype(BF16)
    zsend_q[...] = q_ref[:, oth_cols].astype(F32).T.astype(BF16)

    pl.semaphore_wait(barrier, nctx - 1 + ntp - 1)

    def ring_copy(s, zz, part):
        rows = pl.ds(part * ROWS, ROWS)
        return pltpu.make_async_remote_copy(
            kv.at[s, zz, 0, rows], kv.at[s + 1, zz, 0, rows],
            ring_ss.at[s, zz, part], ring_rs.at[s + 1, zz, part],
            device_id=nxt, device_id_type=MESH)

    def ring_arrival(s, zz, part):
        rows = pl.ds(part * ROWS, ROWS)
        return pltpu.make_async_remote_copy(
            kv.at[s - 1, zz, 0, rows], kv.at[s, zz, 0, rows],
            ring_ss.at[s - 1, zz, part], ring_rs.at[s, zz, part],
            device_id=nxt, device_id_type=MESH)

    def sib_copy(s, zz):
        return pltpu.make_async_remote_copy(
            kv.at[s, zz, 0], kv.at[s, zz, 1], sib_ss.at[s, zz], sib_rs.at[s, zz],
            device_id=sib, device_id_type=MESH)

    def z_copy(i):
        src, dst = ((zsend_kv.at[0:ROWS], kv.at[0, 1, 0, 0:ROWS]),
                    (zsend_kv.at[ROWS:2 * ROWS], kv.at[0, 1, 0, ROWS:2 * ROWS]),
                    (zsend_q, qt.at[1]),
                    (ss_send, ss_recv),
                    (oz_send, oz_recv))[i]
        return pltpu.make_async_remote_copy(
            src, dst, z_ss.at[i], z_rs.at[i], device_id=partner, device_id_type=MESH)

    ring_copy(0, 0, 0).start()
    z_copy(0).start()
    ring_copy(0, 0, 1).start()
    z_copy(1).start()
    z_copy(2).start()
    sib_copy(0, 0).start()

    lane = lax.broadcasted_iota(jnp.int32, (1, ROWS), 1)
    for zz in range(2):
        dev = at(jnp.where(zz == 0, zh, 1 - zh), y, core)
        p0 = bo_ref[dev * NB]
        p1 = bo_ref[dev * NB + 1]
        p2 = bo_ref[dev * NB + 2]
        qpos[zz] = jnp.where(lane < BLK, p0, jnp.where(lane < 2 * BLK, p1, p2))
    mx[...] = jnp.full(mx.shape, NEG, F32)
    acc[...] = jnp.zeros(acc.shape, F32)
    ones = jnp.ones((16, ROWS), BF16)

    def unit(s, zk, zq):
        qtv = qt[zq]
        qv = qpos[zq]
        zsrc = zh if zk == 0 else 1 - zh
        srcs = (at(zsrc, y - step_dir * s, core), at(zsrc, y + step_dir * s, 1 - core))
        tiles = []
        m_old = mx[zq]
        m_new = m_old
        for d in range(2):
            st = jnp.dot(kv[s, zk, d, 0:ROWS], qtv, preferred_element_type=F32)
            for b in range(NB):
                tile = st[b * BLK:(b + 1) * BLK]
                if d == 0 and zk == zq:
                    rel = (lax.broadcasted_iota(jnp.int32, (BLK, BLK), 0)
                           - lax.broadcasted_iota(jnp.int32, (BLK, BLK), 1))
                    limit = jnp.where(s == 0, 0, BLK)
                    cut = jnp.where(rel <= limit, tile[:, b * BLK:(b + 1) * BLK], -jnp.inf)
                    parts = [tile[:, j * BLK:(j + 1) * BLK] if j != b else cut for j in range(NB)]
                    tile = jnp.concatenate(parts, axis=1)
                vis = bo_ref[srcs[d] * NB + b] <= qv
                m_new = jnp.maximum(m_new, jnp.where(vis, jnp.max(tile, axis=0, keepdims=True), NEG))
                tiles.append((tile, vis))
        mc = m_new * EXP_SCALE
        total = acc[zq] * jnp.exp2(m_old * EXP_SCALE - mc)
        for d in range(2):
            probs = []
            vts = []
            for b in range(NB):
                tile, vis = tiles[d * NB + b]
                probs.append(jnp.exp2(tile * EXP_SCALE - jnp.where(vis, mc, jnp.inf)).astype(BF16))
                vts.append(kv[s, zk, d, ROWS + b * BLK:ROWS + (b + 1) * BLK])
            vt = jnp.concatenate([jnp.concatenate(vts, axis=1), ones], axis=0)
            total = total + jnp.dot(vt, jnp.concatenate(probs, axis=0), preferred_element_type=F32)
        acc[zq] = total
        mx[zq] = m_new

    def take(s, zz, part):
        @pl.when(s < ny)
        def _():
            ring_arrival(s, zz, part).wait_recv()

            @pl.when(s < ny - 1)
            def _():
                ring_copy(s, zz, part).start()

            if part == 1:
                sib_copy(s, zz).start()

    @pl.loop(0, ny)
    def _(s):
        take(s + 1, 0, 0)
        sib_copy(s, 0).wait_recv()
        unit(s, 0, 0)
        take(s + 1, 0, 1)

    z_copy(0).wait_recv()
    ring_copy(0, 1, 0).start()
    z_copy(1).wait_recv()
    ring_copy(0, 1, 1).start()
    sib_copy(0, 1).start()
    z_copy(2).wait_recv()

    @pl.loop(0, ny)
    def _(s):
        unit(s, 0, 1)
        take(s + 1, 1, 0)
        sib_copy(s, 1).wait_recv()
        unit(s, 1, 1)
        take(s + 1, 1, 1)

        @pl.when(s >= 1)
        def _():
            unit(s - 1, 1, 0)

    def finish(zq):
        whole = acc[zq]
        out = (whole[0:HD] / whole[HD:HD + 1]).astype(BF16).astype(F32)
        return jnp.sum(out * out, axis=0, keepdims=True), out.T.astype(BF16)

    squares, out = finish(1)
    ss_send[...] = squares
    oz_send[...] = out
    z_copy(3).start()
    z_copy(4).start()
    unit(ny - 1, 1, 0)
    squares, out = finish(0)
    aout_ref[:, own_cols] = out
    z_copy(3).wait_recv()
    sq[pl.ds(tp, 1)] = (squares + ss_recv[...])[None]

    def tp_copy(i, frm):
        return pltpu.make_async_remote_copy(
            sq.at[frm], sq.at[frm], tp_ss.at[i], tp_rs.at[frm],
            device_id=(ctx, lax.rem(tp + i, ntp)), device_id_type=MESH)

    @pl.loop(1, ntp)
    def _(i):
        tp_copy(i, tp).start()

    z_copy(4).wait_recv()
    aout_ref[:, oth_cols] = oz_recv[...]

    @pl.loop(1, ntp)
    def _(i):
        tp_copy(i, lax.rem(tp + i, ntp)).wait_recv()

    square_sum = jnp.sum(sq[...], axis=0)
    scaled = lax.rsqrt(square_sum / (ntp * 2 * HD) + 1e-06)
    scaled = jnp.broadcast_to(scaled, (BLK, ROWS)).T
    for b in range(NB):
        rows = slice(b * BLK, (b + 1) * BLK)
        for g in range(2):
            cols = slice(g * HD, (g + 1) * HD)
            val = (aout_ref[rows, cols].astype(F32) * scaled[rows] * ng_ref[:, cols]
                   * ig_ref[rows, cols].astype(F32)).astype(BF16)
            mixed[rows, cols] = val
            xs[pl.ds(2 * b + g, BLK, stride=8), :] = val.astype(F32)
    for r in (2 * NB, 2 * NB + 1):
        xs[pl.ds(r, BLK, stride=8), :] = jnp.zeros((BLK, HD), F32)

    def x_at(t):
        return xs[pl.ds(pl.multiple_of(t * 8, 8), 8), :]

    dec = [dec_ref[m] for m in range(MODES)]
    zeros = tuple(jnp.zeros((8, HD), F32) for _ in range(MODES))

    def end_step(t, state):
        x = x_at(t)
        return tuple(state[m] * dec[m] + x for m in range(MODES))

    state = lax.fori_loop(0, BLK, end_step, zeros, unroll=4)
    for m in range(MODES):
        ends[m] = state[m]

    def mode_chip(m):
        return 2 * (m // per)

    def end_copy(m, frm):
        return pltpu.make_async_remote_copy(
            ends.at[m], gath.at[lax.rem(m, per), frm], e_ss.at[m], e_rs.at[lax.rem(m, per), frm],
            device_id=(mode_chip(m), tp), device_id_type=MESH)

    @pl.loop(0, MODES)
    def _(m):
        @pl.when(mode_chip(m) != ctx)
        def _():
            end_copy(m, ctx).start()

        @pl.when(mode_chip(m) == ctx)
        def _():
            gath[lax.rem(m, per), ctx] = ends[m]

    def inside_step(t, state):
        x = x_at(t)
        state = tuple(state[m] * dec[m] + x for m in range(MODES))
        terms = [state[m] * wgt_ref[m] for m in range(MODES)]
        while len(terms) > 1:
            terms = [a + b for a, b in zip(terms[::2], terms[1::2])]
        ys[pl.ds(pl.multiple_of(t * 8, 8), 8), :] = terms[0]
        return state

    def reply_copy(mm, to, chip):
        return pltpu.make_async_remote_copy(
            reply.at[mm, to], enter.at[chip * per + mm], r_ss.at[mm, to], r_rs.at[chip * per + mm],
            device_id=(to, tp), device_id_type=MESH)

    @pl.when(core == 0)
    def _():
        chip = ctx // 2

        @pl.loop(0, nctx)
        def _(frm):
            @pl.when(frm != ctx)
            def _():
                for mm in range(per):
                    end_copy(chip * per + mm, frm).wait_recv()

        for mm in range(per):
            mode = chip * per + mm
            blkdec = blkdec_ref[mode]

            def block_step(p, carry):
                prefix[pl.ds(2 * p, 1), :] = carry[0]
                prefix[pl.ds(2 * p + 1, 1), :] = carry[1]
                code = row_of_ref[p]
                return tuple(
                    carry[g] * blkdec[g:g + 1] + gath[mm, code // 8, pl.ds(lax.rem(code, 8) + g, 1), :]
                    for g in range(2))

            start = (jnp.zeros((1, HD), F32), jnp.zeros((1, HD), F32))
            lax.fori_loop(0, nctx * NB, block_step, start, unroll=4)

            @pl.loop(0, nctx)
            def _(to):
                for b in range(NB):
                    pos = bo_ref[to * NB + b]
                    for g in range(2):
                        reply[mm, to, 2 * b + g:2 * b + g + 1] = prefix[pl.ds(2 * pos + g, 1), :]
                reply[mm, to, 2 * NB:8] = jnp.zeros((8 - 2 * NB, HD), F32)

                @pl.when(to != ctx)
                def _():
                    reply_copy(mm, to, chip).start()

                @pl.when(to == ctx)
                def _():
                    enter[chip * per + mm] = reply[mm, to]

    lax.fori_loop(0, BLK, inside_step, zeros, unroll=2)

    @pl.loop(0, half)
    def _(chip):
        @pl.when(2 * chip != ctx)
        def _():
            for mm in range(per):
                reply_copy(mm, ctx, chip).wait_recv()

    def carry_step(t, state):
        state = tuple(state[m] * dec[m] for m in range(MODES))
        terms = list(state)
        while len(terms) > 1:
            terms = [a + b for a, b in zip(terms[::2], terms[1::2])]
        rows = pl.ds(pl.multiple_of(t * 8, 8), 8)
        ys[rows, :] = ys[rows, :] + terms[0]
        return state

    lax.fori_loop(0, BLK, carry_step, tuple(enter[m] * wgt_ref[m] for m in range(MODES)), unroll=4)

    for b in range(NB):
        rows = slice(b * BLK, (b + 1) * BLK)
        for g in range(2):
            cols = slice(g * HD, (g + 1) * HD)
            conv = ys[pl.ds(2 * b + g, BLK, stride=8), :].astype(BF16).astype(F32)
            hout_ref[rows, cols] = (og_ref[rows, cols].astype(F32) * (
                conv + sg_ref[:, cols] * mixed[rows, cols].astype(F32))).astype(BF16)

    @pl.loop(0, ny)
    def _(s):
        for zz in range(2):
            sib_copy(s, zz).wait_send()

            @pl.when(s < ny - 1)
            def _():
                for part in range(2):
                    ring_copy(s, zz, part).wait_send()

    for i in range(5):
        z_copy(i).wait_send()

    @pl.loop(1, ntp)
    def _(i):
        tp_copy(i, tp).wait_send()

    @pl.loop(0, MODES)
    def _(m):
        @pl.when(mode_chip(m) != ctx)
        def _():
            end_copy(m, ctx).wait_send()

    @pl.when(core == 0)
    def _():
        @pl.loop(0, nctx)
        def _(to):
            @pl.when(to != ctx)
            def _():
                for mm in range(per):
                    reply_copy(mm, to, ctx // 2).wait_send()


def per_device(nctx, ntp, queries, keys, values, out_gate, in_gate, norm_gain, skip_gain, rates, residues, block_order):
    ny = nctx // 4
    nblk = block_order.shape[0]
    per = max(1, MODES // (nctx // 2))
    stored = jnp.arange(nblk, dtype=jnp.int32)
    codes = (stored // NB) * 8 + (stored % NB) * 2
    row_of = jnp.sum(jnp.where(block_order[None, :] == stored[:, None], codes[None, :], 0), axis=1)

    def spread(table):
        tiles = table.T.reshape(MODES, 1, 2, HD)
        return jnp.broadcast_to(tiles, (MODES, 4, 2, HD)).reshape(MODES, 8, HD)

    dec = spread(jnp.exp(-rates))
    wgt = spread(residues * jnp.sqrt(-jnp.expm1(-2.0 * rates)))
    blkdec = spread(jnp.exp(-BLK * rates))
    vmem = pl.BlockSpec(memory_space=pltpu.VMEM)
    smem = pl.BlockSpec(memory_space=pltpu.SMEM)
    dma = pltpu.SemaphoreType.DMA
    return pl.pallas_call(
        functools.partial(body, nctx, ntp),
        out_shape=(jax.ShapeDtypeStruct((ROWS, 2 * HD), BF16), jax.ShapeDtypeStruct((ROWS, 2 * HD), BF16)),
        in_specs=[smem, smem] + [vmem] * 10,
        out_specs=(vmem, vmem),
        scratch_shapes=[
            pltpu.VMEM((ny, 2, 2, 2 * ROWS, HD), BF16),
            pltpu.VMEM((2, HD, ROWS), BF16),
            pltpu.VMEM((2 * ROWS, HD), BF16),
            pltpu.VMEM((HD, ROWS), BF16),
            pltpu.VMEM((2, HD + 16, ROWS), F32),
            pltpu.VMEM((2, 1, ROWS), F32),
            pltpu.VMEM((2, 1, ROWS), jnp.int32),
            pltpu.VMEM((ROWS, HD), BF16),
            pltpu.VMEM((ROWS, HD), BF16),
            pltpu.VMEM((1, ROWS), F32),
            pltpu.VMEM((1, ROWS), F32),
            pltpu.VMEM((ntp, 1, ROWS), F32),
            pltpu.VMEM((BLK * 8, HD), F32),
            pltpu.VMEM((BLK * 8, HD), F32),
            pltpu.VMEM((ROWS, 2 * HD), BF16),
            pltpu.VMEM((MODES, 8, HD), F32),
            pltpu.VMEM((per, nctx, 8, HD), F32),
            pltpu.VMEM((2 * nblk, HD), F32),
            pltpu.VMEM((per, nctx, 8, HD), F32),
            pltpu.VMEM((MODES, 8, HD), F32),
            dma((ny, 2, 2)), dma((ny, 2, 2)), dma((ny, 2)), dma((ny, 2)), dma((5,)), dma((5,)),
            dma((ntp,)), dma((ntp,)), dma((MODES,)), dma((per, nctx)), dma((per, nctx)), dma((MODES,)),
        ],
        compiler_params=pltpu.CompilerParams(
            collective_id=0, has_side_effects=True, vmem_limit_bytes=48 * 1024 * 1024),
    )(block_order, row_of, queries, keys, values, out_gate, in_gate,
      norm_gain.reshape(1, -1), skip_gain.reshape(1, -1), dec, wgt, blkdec)


def solution(mesh):
    placed = (
        P("ctx", "tp"),
        P("ctx", "tp"),
        P("ctx", "tp"),
        P("ctx", "tp"),
        P("ctx", "tp"),
        P("tp"),
        P("tp"),
        P("tp", None),
        P("tp", None),
        P(),
    )
    return jax.shard_map(
        functools.partial(per_device, mesh.shape["ctx"], mesh.shape["tp"]),
        mesh=mesh,
        in_specs=placed,
        out_specs=(P("ctx", "tp"), P("ctx", "tp")),
        check_vma=False,
    )
```

```python
import functools
import math

import jax
import jax.numpy as jnp
from jax import lax
from jax.experimental import pallas as pl
from jax.experimental.pallas import tpu as pltpu
from jax.sharding import PartitionSpec as P

HD = 128
BLK = 128
MODES = 16
NB = 3
ROWS = NB * BLK
EXP_SCALE = math.log2(math.e) / math.sqrt(HD)
NEG = -1e30
MESH = pl.DeviceIdType.MESH
F32 = jnp.float32
BF16 = jnp.bfloat16


def body(
    nctx, ntp,
    bo_in,    q_in, k_in, v_in, og_in, ig_in, ng_in, sg_in, rates_in, residues_in,
    aout_ref, hout_ref,
    kv, qt, zsend_kv, zsend_q, acc, mx, qpos,
    oz_send, oz_recv, ss_send, ss_recv, sq, xs, ys, mixed,
    ends, gath, prefix, reply, enter,
    q_ref, k_ref, v_ref, og_ref, ig_ref, ng_ref, sg_ref, rates, residues, bo_ref, row_vec, row_of_ref,
    dec_ref, wgt_ref, blkdec_ref, in_sem, row_sem,
    plus_ss, plus_rs, minus_ss, minus_rs, sib_ss, sib_rs, z_ss, z_rs, tp_ss, tp_rs, e_ss, e_rs, r_ss, r_rs,
):
    ny = nctx // 4
    half = nctx // 2
    per = MODES // half if MODES >= half else 1
    ctx = lax.axis_index("ctx")
    tp = lax.axis_index("tp")
    core = lax.rem(ctx, 2)
    y = lax.rem(ctx // 2, ny)
    zh = ctx // half
    hs = ny // 2

    def at(z, yy, c):
        return z * half + lax.rem(yy + 2 * ny, ny) * 2 + c

    after = (at(zh, y + 1, core), tp)
    before = (at(zh, y - 1, core), tp)
    sib = (at(zh, y, 1 - core), tp)
    partner = (lax.rem(ctx + half, nctx), tp)

    loads = [
        pltpu.make_async_copy(src, dst, in_sem.at[i])
        for i, (src, dst) in enumerate((
            (v_in, v_ref), (k_in, k_ref), (q_in, q_ref), (bo_in, bo_ref), (rates_in, rates),
            (residues_in, residues), (ng_in, ng_ref), (sg_in, sg_ref), (ig_in, ig_ref), (og_in, og_ref)))]
    for load in loads:
        load.start()
    barrier = pltpu.get_barrier_semaphore()

    @pl.loop(1, nctx)
    def _(i):
        pl.semaphore_signal(barrier, inc=1, device_id=(lax.rem(ctx + i, nctx), tp), device_id_type=MESH)

    @pl.loop(1, ntp)
    def _(i):
        pl.semaphore_signal(barrier, inc=1, device_id=(ctx, lax.rem(tp + i, ntp)), device_id_type=MESH)

    own_cols = pl.ds(pl.multiple_of(zh * HD, HD), HD)
    oth_cols = pl.ds(pl.multiple_of((1 - zh) * HD, HD), HD)

    def put_kv(dst, cols):
        dst[0:ROWS, :] = k_ref[:, cols]
        for b in range(NB):
            blk = v_ref[b * BLK:(b + 1) * BLK, cols].astype(F32)
            dst[ROWS + b * BLK:ROWS + (b + 1) * BLK, :] = blk.T.astype(BF16)

    for load in loads[:3]:
        load.wait()
    put_kv(kv.at[0, 0, 0], own_cols)
    put_kv(zsend_kv, oth_cols)
    qt[0] = q_ref[:, own_cols].astype(F32).T.astype(BF16)
    zsend_q[...] = q_ref[:, oth_cols].astype(F32).T.astype(BF16)

    pl.semaphore_wait(barrier, nctx - 1 + ntp - 1)

    def plus_copy(j, zz, part):
        rows = pl.ds(part * ROWS, ROWS)
        return pltpu.make_async_remote_copy(
            kv.at[j, zz, 0, rows], kv.at[j + 1, zz, 0, rows],
            plus_ss.at[j, zz, part], plus_rs.at[j, zz, part],
            device_id=after, device_id_type=MESH)

    def minus_copy(j, zz, part):
        rows = pl.ds(part * ROWS, ROWS)
        return pltpu.make_async_remote_copy(
            kv.at[lax.rem(ny - j, ny), zz, 0, rows], kv.at[ny - 1 - j, zz, 0, rows],
            minus_ss.at[j, zz, part], minus_rs.at[j, zz, part],
            device_id=before, device_id_type=MESH)

    def launch(zz, part):
        if part == 0 or hs > 1:
            plus_copy(0, zz, part).start()
        if part == 1 or hs > 1:
            minus_copy(0, zz, part).start()

    def sib_copy(s, zz):
        return pltpu.make_async_remote_copy(
            kv.at[s, zz, 0], kv.at[s, zz, 1], sib_ss.at[s, zz], sib_rs.at[s, zz],
            device_id=sib, device_id_type=MESH)

    def z_copy(i):
        src, dst = ((zsend_kv.at[0:ROWS], kv.at[0, 1, 0, 0:ROWS]),
                    (zsend_kv.at[ROWS:2 * ROWS], kv.at[0, 1, 0, ROWS:2 * ROWS]),
                    (zsend_q, qt.at[1]),
                    (ss_send, ss_recv),
                    (oz_send, oz_recv))[i]
        return pltpu.make_async_remote_copy(
            src, dst, z_ss.at[i], z_rs.at[i], device_id=partner, device_id_type=MESH)

    launch(0, 0)
    z_copy(2).start()
    launch(0, 1)
    sib_copy(0, 0).start()
    z_copy(0).start()
    z_copy(1).start()

    for load in loads[3:6]:
        load.wait()
    lane = lax.broadcasted_iota(jnp.int32, (1, ROWS), 1)
    for zz in range(2):
        dev = at(jnp.where(zz == 0, zh, 1 - zh), y, core)
        p0 = bo_ref[dev * NB]
        p1 = bo_ref[dev * NB + 1]
        p2 = bo_ref[dev * NB + 2]
        qpos[zz] = jnp.where(lane < BLK, p0, jnp.where(lane < 2 * BLK, p1, p2))
    mx[...] = jnp.full(mx.shape, NEG, F32)
    acc[...] = jnp.zeros(acc.shape, F32)
    ones = jnp.ones((16, 2 * ROWS), BF16)

    def unit(j, zk, zqs=(0, 1)):
        qtv = jnp.concatenate([qt[zq] for zq in zqs], axis=1)
        qv = jnp.concatenate([qpos[zq] for zq in zqs], axis=1)
        m_old = jnp.concatenate([mx[zq] for zq in zqs], axis=1)
        zsrc = zh if zk == 0 else 1 - zh
        srcs = (at(zsrc, y - j, core), at(zsrc, y - j, 1 - core))
        tiles = []
        m_new = m_old
        for d in range(2):
            st = jnp.dot(kv[j, zk, d, 0:ROWS], qtv, preferred_element_type=F32)
            for b in range(NB):
                tile = st[b * BLK:(b + 1) * BLK]
                if d == 0 and zk in zqs:
                    rel = (lax.broadcasted_iota(jnp.int32, (BLK, BLK), 0)
                           - lax.broadcasted_iota(jnp.int32, (BLK, BLK), 1))
                    limit = jnp.where(j == 0, 0, BLK)
                    spot = zqs.index(zk) * NB + b
                    parts = [tile[:, i * BLK:(i + 1) * BLK] for i in range(NB * len(zqs))]
                    parts[spot] = jnp.where(rel <= limit, parts[spot], -jnp.inf)
                    tile = jnp.concatenate(parts, axis=1)
                vis = bo_ref[srcs[d] * NB + b] <= qv
                m_new = jnp.maximum(m_new, jnp.where(vis, jnp.max(tile, axis=0, keepdims=True), NEG))
                tiles.append((tile, vis))
        mc = m_new * EXP_SCALE
        probs = [
            jnp.exp2(tile * EXP_SCALE - jnp.where(vis, mc, jnp.inf)).astype(BF16) for tile, vis in tiles]
        vts = [
            kv[j, zk, d, ROWS + b * BLK:ROWS + (b + 1) * BLK] for d in range(2) for b in range(NB)]
        vt = jnp.concatenate([jnp.concatenate(vts, axis=1), ones], axis=0)
        summed = jnp.dot(vt, jnp.concatenate(probs, axis=0), preferred_element_type=F32)
        scale = jnp.exp2(m_old * EXP_SCALE - mc)
        for i, zq in enumerate(zqs):
            cols = slice(i * ROWS, (i + 1) * ROWS)
            acc[zq] = acc[zq] * scale[:, cols] + summed[:, cols]
            mx[zq] = m_new[:, cols]

    def take(t, zz, part):
        far = hs + 1 if part == 0 else hs
        near = hs + 1 if part == 1 else hs

        @pl.when(t < far)
        def _():
            plus_copy(t - 1, zz, part).wait_recv()

            @pl.when(t + 1 < far)
            def _():
                plus_copy(t, zz, part).start()

        @pl.when(t < near)
        def _():
            minus_copy(t - 1, zz, part).wait_recv()

            @pl.when(t + 1 < near)
            def _():
                minus_copy(t, zz, part).start()

        if part == 1:
            sib_copy(t, zz).start()

            @pl.when(t < hs)
            def _():
                sib_copy(ny - t, zz).start()

    def walk(zz):
        @pl.loop(0, hs)
        def _(s):
            take(s + 1, zz, 0)
            sib_copy(s, zz).wait_recv()
            unit(s, zz)
            take(s + 1, zz, 1)

            @pl.when(s > 0)
            def _():
                sib_copy(ny - s, zz).wait_recv()
                unit(ny - s, zz)

    nblk = nctx * NB
    spot = lax.broadcasted_iota(jnp.int32, (1, BLK), 1)

    def place(i, codes):
        code = lax.div(i, NB) * 8 + lax.rem(i, NB) * 2
        return jnp.where(spot == bo_ref[i], code, codes)

    row_vec[...] = lax.fori_loop(0, nblk, place, jnp.zeros((1, BLK), jnp.int32), unroll=4)
    row_copy = pltpu.make_async_copy(row_vec, row_of_ref, row_sem.at[0])
    row_copy.start()
    even = lax.rem(lax.broadcasted_iota(jnp.int32, (8, HD), 0), 2) == 0

    @pl.loop(0, MODES)
    def _(m):
        def pair(ref):
            row = ref[pl.ds(m, 1), :]
            return jnp.where(even, row[:, 0:HD], row[:, HD:2 * HD])

        rate = pair(rates)
        two = 2.0 * rate
        series = 1.0 - two * (1 / 6)
        for k in (5, 4, 3, 2):
            series = 1.0 - two * series * (1 / k)
        dec_ref[m] = jnp.exp(-rate)
        blkdec_ref[m] = jnp.exp(-BLK * rate)
        wgt_ref[m] = pair(residues) * jnp.sqrt(two * series)

    row_copy.wait()
    z_copy(2).wait_recv()
    walk(0)
    z_copy(0).wait_recv()
    launch(1, 0)
    z_copy(1).wait_recv()
    launch(1, 1)
    sib_copy(0, 1).start()
    sib_copy(hs, 0).wait_recv()
    unit(hs, 0)
    walk(1)
    sib_copy(hs, 1).wait_recv()
    unit(hs, 1, (1,))

    def finish(zq):
        whole = acc[zq]
        out = (whole[0:HD] / whole[HD:HD + 1]).astype(BF16).astype(F32)
        return jnp.sum(out * out, axis=0, keepdims=True), out.T.astype(BF16)

    squares, out = finish(1)
    ss_send[...] = squares
    oz_send[...] = out
    z_copy(3).start()
    z_copy(4).start()
    unit(hs, 1, (0,))
    squares, out = finish(0)
    aout_ref[:, own_cols] = out
    z_copy(3).wait_recv()
    sq[pl.ds(tp, 1)] = (squares + ss_recv[...])[None]

    def tp_copy(i, frm):
        return pltpu.make_async_remote_copy(
            sq.at[frm], sq.at[frm], tp_ss.at[i], tp_rs.at[frm],
            device_id=(ctx, lax.rem(tp + i, ntp)), device_id_type=MESH)

    @pl.loop(1, ntp)
    def _(i):
        tp_copy(i, tp).start()

    z_copy(4).wait_recv()
    aout_ref[:, oth_cols] = oz_recv[...]

    @pl.loop(1, ntp)
    def _(i):
        tp_copy(i, lax.rem(tp + i, ntp)).wait_recv()

    for load in loads[6:]:
        load.wait()
    square_sum = jnp.sum(sq[...], axis=0)
    scaled = lax.rsqrt(square_sum / (ntp * 2 * HD) + 1e-06)
    scaled = jnp.broadcast_to(scaled, (BLK, ROWS)).T
    for b in range(NB):
        rows = slice(b * BLK, (b + 1) * BLK)
        for g in range(2):
            cols = slice(g * HD, (g + 1) * HD)
            val = (aout_ref[rows, cols].astype(F32) * scaled[rows] * ng_ref[:, cols]
                   * ig_ref[rows, cols].astype(F32)).astype(BF16)
            mixed[rows, cols] = val
            xs[pl.ds(2 * b + g, BLK, stride=8), :] = val.astype(F32)
    for r in (2 * NB, 2 * NB + 1):
        xs[pl.ds(r, BLK, stride=8), :] = jnp.zeros((BLK, HD), F32)

    def x_at(t):
        return xs[pl.ds(pl.multiple_of(t * 8, 8), 8), :]

    dec = [dec_ref[m] for m in range(MODES)]
    zeros = tuple(jnp.zeros((8, HD), F32) for _ in range(MODES))

    def end_step(t, state):
        x = x_at(t)
        return tuple(state[m] * dec[m] + x for m in range(MODES))

    state = lax.fori_loop(0, BLK, end_step, zeros, unroll=4)
    for m in range(MODES):
        ends[m] = state[m]

    def mode_chip(m):
        return 2 * (m // per)

    def end_copy(m, frm):
        return pltpu.make_async_remote_copy(
            ends.at[m], gath.at[lax.rem(m, per), frm], e_ss.at[m], e_rs.at[lax.rem(m, per), frm],
            device_id=(mode_chip(m), tp), device_id_type=MESH)

    @pl.loop(0, MODES)
    def _(m):
        @pl.when(mode_chip(m) != ctx)
        def _():
            end_copy(m, ctx).start()

        @pl.when(mode_chip(m) == ctx)
        def _():
            gath[lax.rem(m, per), ctx] = ends[m]

    def inside_step(t, state):
        x = x_at(t)
        state = tuple(state[m] * dec[m] + x for m in range(MODES))
        terms = [state[m] * wgt_ref[m] for m in range(MODES)]
        while len(terms) > 1:
            terms = [a + b for a, b in zip(terms[::2], terms[1::2])]
        ys[pl.ds(pl.multiple_of(t * 8, 8), 8), :] = terms[0]
        return state

    def reply_copy(mm, to, chip):
        return pltpu.make_async_remote_copy(
            reply.at[mm, to], enter.at[chip * per + mm], r_ss.at[mm, to], r_rs.at[chip * per + mm],
            device_id=(to, tp), device_id_type=MESH)

    @pl.when(core == 0)
    def _():
        chip = ctx // 2

        @pl.loop(0, nctx)
        def _(frm):
            @pl.when(frm != ctx)
            def _():
                for mm in range(per):
                    end_copy(chip * per + mm, frm).wait_recv()

        for mm in range(per):
            mode = chip * per + mm
            blkdec = blkdec_ref[mode]

            def block_step(p, carry):
                prefix[pl.ds(2 * p, 1), :] = carry[0]
                prefix[pl.ds(2 * p + 1, 1), :] = carry[1]
                code = row_of_ref[0, p]
                return tuple(
                    carry[g] * blkdec[g:g + 1] + gath[mm, code // 8, pl.ds(lax.rem(code, 8) + g, 1), :]
                    for g in range(2))

            start = (jnp.zeros((1, HD), F32), jnp.zeros((1, HD), F32))
            lax.fori_loop(0, nctx * NB, block_step, start, unroll=4)

            @pl.loop(0, nctx)
            def _(to):
                for b in range(NB):
                    pos = bo_ref[to * NB + b]
                    for g in range(2):
                        reply[mm, to, 2 * b + g:2 * b + g + 1] = prefix[pl.ds(2 * pos + g, 1), :]
                reply[mm, to, 2 * NB:8] = jnp.zeros((8 - 2 * NB, HD), F32)

                @pl.when(to != ctx)
                def _():
                    reply_copy(mm, to, chip).start()

                @pl.when(to == ctx)
                def _():
                    enter[chip * per + mm] = reply[mm, to]

    lax.fori_loop(0, BLK, inside_step, zeros, unroll=2)

    @pl.loop(0, half)
    def _(chip):
        @pl.when(2 * chip != ctx)
        def _():
            for mm in range(per):
                reply_copy(mm, ctx, chip).wait_recv()

    def carry_step(t, state):
        state = tuple(state[m] * dec[m] for m in range(MODES))
        terms = list(state)
        while len(terms) > 1:
            terms = [a + b for a, b in zip(terms[::2], terms[1::2])]
        rows = pl.ds(pl.multiple_of(t * 8, 8), 8)
        ys[rows, :] = ys[rows, :] + terms[0]
        return state

    lax.fori_loop(0, BLK, carry_step, tuple(enter[m] * wgt_ref[m] for m in range(MODES)), unroll=4)

    for b in range(NB):
        rows = slice(b * BLK, (b + 1) * BLK)
        for g in range(2):
            cols = slice(g * HD, (g + 1) * HD)
            conv = ys[pl.ds(2 * b + g, BLK, stride=8), :].astype(BF16).astype(F32)
            hout_ref[rows, cols] = (og_ref[rows, cols].astype(F32) * (
                conv + sg_ref[:, cols] * mixed[rows, cols].astype(F32))).astype(BF16)

    @pl.loop(0, ny)
    def _(j):
        for zz in range(2):
            sib_copy(j, zz).wait_send()

    @pl.loop(0, hs)
    def _(j):
        for zz in range(2):
            plus_copy(j, zz, 0).wait_send()
            minus_copy(j, zz, 1).wait_send()

            @pl.when(j < hs - 1)
            def _():
                plus_copy(j, zz, 1).wait_send()
                minus_copy(j, zz, 0).wait_send()

    for i in range(5):
        z_copy(i).wait_send()

    @pl.loop(1, ntp)
    def _(i):
        tp_copy(i, tp).wait_send()

    @pl.loop(0, MODES)
    def _(m):
        @pl.when(mode_chip(m) != ctx)
        def _():
            end_copy(m, ctx).wait_send()

    @pl.when(core == 0)
    def _():
        @pl.loop(0, nctx)
        def _(to):
            @pl.when(to != ctx)
            def _():
                for mm in range(per):
                    reply_copy(mm, to, ctx // 2).wait_send()


def per_device(nctx, ntp, queries, keys, values, out_gate, in_gate, norm_gain, skip_gain, rates, residues, block_order):
    ny = nctx // 4
    nblk = block_order.shape[0]
    per = max(1, MODES // (nctx // 2))
    vmem = pl.BlockSpec(memory_space=pltpu.VMEM)
    hbm = pl.BlockSpec(memory_space=pltpu.HBM)
    dma = pltpu.SemaphoreType.DMA
    return pl.pallas_call(
        functools.partial(body, nctx, ntp),
        out_shape=(jax.ShapeDtypeStruct((ROWS, 2 * HD), BF16), jax.ShapeDtypeStruct((ROWS, 2 * HD), BF16)),
        in_specs=[hbm] * 10,
        out_specs=(vmem, vmem),
        scratch_shapes=[
            pltpu.VMEM((ny, 2, 2, 2 * ROWS, HD), BF16),
            pltpu.VMEM((2, HD, ROWS), BF16),
            pltpu.VMEM((2 * ROWS, HD), BF16),
            pltpu.VMEM((HD, ROWS), BF16),
            pltpu.VMEM((2, HD + 16, ROWS), F32),
            pltpu.VMEM((2, 1, ROWS), F32),
            pltpu.VMEM((2, 1, ROWS), jnp.int32),
            pltpu.VMEM((ROWS, HD), BF16),
            pltpu.VMEM((ROWS, HD), BF16),
            pltpu.VMEM((1, ROWS), F32),
            pltpu.VMEM((1, ROWS), F32),
            pltpu.VMEM((ntp, 1, ROWS), F32),
            pltpu.VMEM((BLK * 8, HD), F32),
            pltpu.VMEM((BLK * 8, HD), F32),
            pltpu.VMEM((ROWS, 2 * HD), BF16),
            pltpu.VMEM((MODES, 8, HD), F32),
            pltpu.VMEM((per, nctx, 8, HD), F32),
            pltpu.VMEM((2 * nblk, HD), F32),
            pltpu.VMEM((per, nctx, 8, HD), F32),
            pltpu.VMEM((MODES, 8, HD), F32),
            *[pltpu.VMEM((ROWS, 2 * HD), BF16)] * 5, *[pltpu.VMEM((1, 2 * HD), F32)] * 2,
            *[pltpu.VMEM((MODES, 2 * HD), F32)] * 2, pltpu.SMEM((nblk,), jnp.int32),
            pltpu.VMEM((1, BLK), jnp.int32), pltpu.SMEM((1, BLK), jnp.int32),
            *[pltpu.VMEM((MODES, 8, HD), F32)] * 3, dma((10,)), dma((1,)),
            dma((ny // 2, 2, 2)), dma((ny // 2, 2, 2)), dma((ny // 2, 2, 2)), dma((ny // 2, 2, 2)),
            dma((ny, 2)), dma((ny, 2)), dma((5,)), dma((5,)),
            dma((ntp,)), dma((ntp,)), dma((MODES,)), dma((per, nctx)), dma((per, nctx)), dma((MODES,)),
        ],
        compiler_params=pltpu.CompilerParams(
            collective_id=0, has_side_effects=True, vmem_limit_bytes=62 * 1024 * 1024),
    )(block_order, queries, keys, values, out_gate, in_gate,
      norm_gain.reshape(1, -1), skip_gain.reshape(1, -1), rates.T, residues.T)


def solution(mesh):
    placed = (
        P("ctx", "tp"),
        P("ctx", "tp"),
        P("ctx", "tp"),
        P("ctx", "tp"),
        P("ctx", "tp"),
        P("tp"),
        P("tp"),
        P("tp", None),
        P("tp", None),
        P(),
    )
    return jax.shard_map(
        functools.partial(per_device, mesh.shape["ctx"], mesh.shape["tp"]),
        mesh=mesh,
        in_specs=placed,
        out_specs=(P("ctx", "tp"), P("ctx", "tp")),
        check_vma=False,
    )
```

```python
import functools
import math

import jax
import jax.numpy as jnp
from jax import lax
from jax.experimental import pallas as pl
from jax.experimental.pallas import tpu as pltpu
from jax.sharding import PartitionSpec as P

HD = 128
BLK = 128
MODES = 16
NB = 3
ROWS = NB * BLK
EXP_SCALE = math.log2(math.e) / math.sqrt(HD)
NEG = -1e30
MESH = pl.DeviceIdType.MESH
F32 = jnp.float32
BF16 = jnp.bfloat16


def body(
    nctx, ntp,
    bo_in,    q_in, k_in, v_in, og_in, ig_in, ng_in, sg_in, rates_in, residues_in,
    aout_ref, hout_ref,
    kv, qt, zsend_kv, zsend_q, acc, mx, qpos,
    oz_send, oz_recv, ss_send, ss_recv, sq, xs, ys, mixed,
    ends, gath, prefix, reply, enter,
    q_ref, k_ref, v_ref, og_ref, ig_ref, ng_ref, sg_ref, rates, residues, bo_ref, row_vec, row_of_ref,
    dec_ref, wgt_ref, blkdec_ref, in_sem, row_sem,
    plus_ss, plus_rs, minus_ss, minus_rs, sib_ss, sib_rs, z_ss, z_rs, tp_ss, tp_rs, e_ss, e_rs, r_ss, r_rs,
):
    ny = nctx // 4
    half = nctx // 2
    per = MODES // half if MODES >= half else 1
    ctx = lax.axis_index("ctx")
    tp = lax.axis_index("tp")
    core = lax.rem(ctx, 2)
    y = lax.rem(ctx // 2, ny)
    zh = ctx // half
    hs = ny // 2

    def at(z, yy, c):
        return z * half + lax.rem(yy + 2 * ny, ny) * 2 + c

    after = (at(zh, y + 1, core), tp)
    before = (at(zh, y - 1, core), tp)
    sib = (at(zh, y, 1 - core), tp)
    partner = (lax.rem(ctx + half, nctx), tp)

    loads = [
        pltpu.make_async_copy(src, dst, in_sem.at[i])
        for i, (src, dst) in enumerate((
            (v_in, v_ref), (k_in, k_ref), (q_in, q_ref), (bo_in, bo_ref), (rates_in, rates),
            (residues_in, residues), (ng_in, ng_ref), (sg_in, sg_ref), (ig_in, ig_ref), (og_in, og_ref)))]
    for load in loads:
        load.start()
    barrier = pltpu.get_barrier_semaphore()

    @pl.loop(1, nctx)
    def _(i):
        pl.semaphore_signal(barrier, inc=1, device_id=(lax.rem(ctx + i, nctx), tp), device_id_type=MESH)

    @pl.loop(1, ntp)
    def _(i):
        pl.semaphore_signal(barrier, inc=1, device_id=(ctx, lax.rem(tp + i, ntp)), device_id_type=MESH)

    own_cols = pl.ds(pl.multiple_of(zh * HD, HD), HD)
    oth_cols = pl.ds(pl.multiple_of((1 - zh) * HD, HD), HD)

    def put_kv(dst, cols):
        dst[0:ROWS, :] = k_ref[:, cols]
        for b in range(NB):
            blk = v_ref[b * BLK:(b + 1) * BLK, cols].astype(F32)
            dst[ROWS + b * BLK:ROWS + (b + 1) * BLK, :] = blk.T.astype(BF16)

    for load in loads[:3]:
        load.wait()
    put_kv(kv.at[0, 0, 0], own_cols)
    put_kv(zsend_kv, oth_cols)
    qt[0] = q_ref[:, own_cols].astype(F32).T.astype(BF16)
    zsend_q[...] = q_ref[:, oth_cols].astype(F32).T.astype(BF16)

    pl.semaphore_wait(barrier, nctx - 1 + ntp - 1)

    def plus_copy(j, zz, part):
        rows = pl.ds(part * ROWS, ROWS)
        return pltpu.make_async_remote_copy(
            kv.at[j, zz, 0, rows], kv.at[j + 1, zz, 0, rows],
            plus_ss.at[j, zz, part], plus_rs.at[j, zz, part],
            device_id=after, device_id_type=MESH)

    def minus_copy(j, zz, part):
        rows = pl.ds(part * ROWS, ROWS)
        return pltpu.make_async_remote_copy(
            kv.at[lax.rem(ny - j, ny), zz, 0, rows], kv.at[ny - 1 - j, zz, 0, rows],
            minus_ss.at[j, zz, part], minus_rs.at[j, zz, part],
            device_id=before, device_id_type=MESH)

    def launch(zz, part):
        if part == 0 or hs > 1:
            plus_copy(0, zz, part).start()
        if part == 1 or hs > 1:
            minus_copy(0, zz, part).start()

    def sib_copy(s, zz):
        return pltpu.make_async_remote_copy(
            kv.at[s, zz, 0], kv.at[s, zz, 1], sib_ss.at[s, zz], sib_rs.at[s, zz],
            device_id=sib, device_id_type=MESH)

    def z_copy(i):
        src, dst = ((zsend_kv.at[0:ROWS], kv.at[0, 1, 0, 0:ROWS]),
                    (zsend_kv.at[ROWS:2 * ROWS], kv.at[0, 1, 0, ROWS:2 * ROWS]),
                    (zsend_q, qt.at[1]),
                    (ss_send, ss_recv),
                    (oz_send, oz_recv))[i]
        return pltpu.make_async_remote_copy(
            src, dst, z_ss.at[i], z_rs.at[i], device_id=partner, device_id_type=MESH)

    launch(0, 0)
    z_copy(2).start()
    launch(0, 1)
    sib_copy(0, 0).start()
    z_copy(0).start()
    z_copy(1).start()

    for load in loads[3:6]:
        load.wait()
    lane = lax.broadcasted_iota(jnp.int32, (1, ROWS), 1)
    for zz in range(2):
        dev = at(jnp.where(zz == 0, zh, 1 - zh), y, core)
        p0 = bo_ref[dev * NB]
        p1 = bo_ref[dev * NB + 1]
        p2 = bo_ref[dev * NB + 2]
        qpos[zz] = jnp.where(lane < BLK, p0, jnp.where(lane < 2 * BLK, p1, p2))
    mx[...] = jnp.full(mx.shape, NEG, F32)
    acc[...] = jnp.zeros(acc.shape, F32)
    ones = jnp.ones((16, 2 * ROWS), BF16)

    def unit(j, zk, zqs=(0, 1)):
        qtv = jnp.concatenate([qt[zq] for zq in zqs], axis=1)
        qv = jnp.concatenate([qpos[zq] for zq in zqs], axis=1)
        m_old = jnp.concatenate([mx[zq] for zq in zqs], axis=1)
        zsrc = zh if zk == 0 else 1 - zh
        srcs = (at(zsrc, y - j, core), at(zsrc, y - j, 1 - core))
        tiles = []
        m_new = m_old
        for d in range(2):
            st = jnp.dot(kv[j, zk, d, 0:ROWS], qtv, preferred_element_type=F32)
            for b in range(NB):
                tile = st[b * BLK:(b + 1) * BLK]
                if d == 0 and zk in zqs:
                    rel = (lax.broadcasted_iota(jnp.int32, (BLK, BLK), 0)
                           - lax.broadcasted_iota(jnp.int32, (BLK, BLK), 1))
                    limit = jnp.where(j == 0, 0, BLK)
                    spot = zqs.index(zk) * NB + b
                    parts = [tile[:, i * BLK:(i + 1) * BLK] for i in range(NB * len(zqs))]
                    parts[spot] = jnp.where(rel <= limit, parts[spot], -jnp.inf)
                    tile = jnp.concatenate(parts, axis=1)
                vis = bo_ref[srcs[d] * NB + b] <= qv
                m_new = jnp.maximum(m_new, jnp.where(vis, jnp.max(tile, axis=0, keepdims=True), NEG))
                tiles.append((tile, vis))
        mc = m_new * EXP_SCALE
        probs = [
            jnp.exp2(tile * EXP_SCALE - jnp.where(vis, mc, jnp.inf)).astype(BF16) for tile, vis in tiles]
        vts = [
            kv[j, zk, d, ROWS + b * BLK:ROWS + (b + 1) * BLK] for d in range(2) for b in range(NB)]
        vt = jnp.concatenate([jnp.concatenate(vts, axis=1), ones], axis=0)
        summed = jnp.dot(vt, jnp.concatenate(probs, axis=0), preferred_element_type=F32)
        scale = jnp.exp2(m_old * EXP_SCALE - mc)
        for i, zq in enumerate(zqs):
            cols = slice(i * ROWS, (i + 1) * ROWS)
            acc[zq] = acc[zq] * scale[:, cols] + summed[:, cols]
            mx[zq] = m_new[:, cols]

    def take(t, zz, part):
        far = hs + 1 if part == 0 else hs
        near = hs + 1 if part == 1 else hs

        @pl.when(t < far)
        def _():
            plus_copy(t - 1, zz, part).wait_recv()

            @pl.when(t + 1 < far)
            def _():
                plus_copy(t, zz, part).start()

        @pl.when(t < near)
        def _():
            minus_copy(t - 1, zz, part).wait_recv()

            @pl.when(t + 1 < near)
            def _():
                minus_copy(t, zz, part).start()

        if part == 1:
            sib_copy(t, zz).start()

            @pl.when(t < hs)
            def _():
                sib_copy(ny - t, zz).start()

    take(1, 0, 0)
    nblk = nctx * NB
    spot = lax.broadcasted_iota(jnp.int32, (1, BLK), 1)

    def place(i, codes):
        code = lax.div(i, NB) * 8 + lax.rem(i, NB) * 2
        return jnp.where(spot == bo_ref[i], code, codes)

    row_vec[...] = lax.fori_loop(0, nblk, place, jnp.zeros((1, BLK), jnp.int32), unroll=4)
    row_copy = pltpu.make_async_copy(row_vec, row_of_ref, row_sem.at[0])
    row_copy.start()
    take(1, 0, 1)
    even = lax.rem(lax.broadcasted_iota(jnp.int32, (8, HD), 0), 2) == 0

    @pl.loop(0, MODES)
    def _(m):
        def pair(ref):
            row = ref[pl.ds(m, 1), :]
            return jnp.where(even, row[:, 0:HD], row[:, HD:2 * HD])

        rate = pair(rates)
        two = 2.0 * rate
        series = 1.0 - two * (1 / 6)
        for k in (5, 4, 3, 2):
            series = 1.0 - two * series * (1 / k)
        dec_ref[m] = jnp.exp(-rate)
        blkdec_ref[m] = jnp.exp(-BLK * rate)
        wgt_ref[m] = pair(residues) * jnp.sqrt(two * series)

    row_copy.wait()
    z_copy(2).wait_recv()

    def attend(j, zz):
        sib_copy(j, zz).wait_recv()
        unit(j, zz)

    @pl.loop(0, hs - 1)
    def _(s):
        take(s + 2, 0, 0)
        attend(s, 0)
        take(s + 2, 0, 1)

        @pl.when(s > 0)
        def _():
            attend(ny - s, 0)

    z_copy(0).wait_recv()
    launch(1, 0)
    z_copy(1).wait_recv()
    launch(1, 1)
    sib_copy(0, 1).start()

    @pl.loop(hs - 1, min(hs + 2, ny))
    def _(j):
        attend(j, 0)

    @pl.loop(0, hs)
    def _(s):
        take(s + 1, 1, 0)
        attend(s, 1)
        take(s + 1, 1, 1)

        @pl.when(s > 0)
        def _():
            attend(ny - s, 1)

    sib_copy(hs, 1).wait_recv()
    unit(hs, 1, (1,))

    def finish(zq):
        whole = acc[zq]
        out = (whole[0:HD] / whole[HD:HD + 1]).astype(BF16).astype(F32)
        return jnp.sum(out * out, axis=0, keepdims=True), out.T.astype(BF16)

    squares, out = finish(1)
    ss_send[...] = squares
    oz_send[...] = out
    z_copy(3).start()
    z_copy(4).start()
    unit(hs, 1, (0,))
    squares, out = finish(0)
    aout_ref[:, own_cols] = out
    z_copy(3).wait_recv()
    sq[pl.ds(tp, 1)] = (squares + ss_recv[...])[None]

    def tp_copy(i, frm):
        return pltpu.make_async_remote_copy(
            sq.at[frm], sq.at[frm], tp_ss.at[i], tp_rs.at[frm],
            device_id=(ctx, lax.rem(tp + i, ntp)), device_id_type=MESH)

    @pl.loop(1, ntp)
    def _(i):
        tp_copy(i, tp).start()

    z_copy(4).wait_recv()
    aout_ref[:, oth_cols] = oz_recv[...]

    @pl.loop(1, ntp)
    def _(i):
        tp_copy(i, lax.rem(tp + i, ntp)).wait_recv()

    for load in loads[6:]:
        load.wait()
    square_sum = jnp.sum(sq[...], axis=0)
    scaled = lax.rsqrt(square_sum / (ntp * 2 * HD) + 1e-06)
    scaled = jnp.broadcast_to(scaled, (BLK, ROWS)).T
    for b in range(NB):
        rows = slice(b * BLK, (b + 1) * BLK)
        for g in range(2):
            cols = slice(g * HD, (g + 1) * HD)
            val = (aout_ref[rows, cols].astype(F32) * scaled[rows] * ng_ref[:, cols]
                   * ig_ref[rows, cols].astype(F32)).astype(BF16)
            mixed[rows, cols] = val
            xs[pl.ds(2 * b + g, BLK, stride=8), :] = val.astype(F32)
    for r in (2 * NB, 2 * NB + 1):
        xs[pl.ds(r, BLK, stride=8), :] = jnp.zeros((BLK, HD), F32)

    def x_at(t):
        return xs[pl.ds(pl.multiple_of(t * 8, 8), 8), :]

    dec = [dec_ref[m] for m in range(MODES)]
    zeros = tuple(jnp.zeros((8, HD), F32) for _ in range(MODES))

    def end_step(t, state):
        x = x_at(t)
        return tuple(state[m] * dec[m] + x for m in range(MODES))

    state = lax.fori_loop(0, BLK, end_step, zeros, unroll=4)
    for m in range(MODES):
        ends[m] = state[m]

    def mode_chip(m):
        return 2 * (m // per)

    def end_copy(m, frm):
        return pltpu.make_async_remote_copy(
            ends.at[m], gath.at[lax.rem(m, per), frm], e_ss.at[m], e_rs.at[lax.rem(m, per), frm],
            device_id=(mode_chip(m), tp), device_id_type=MESH)

    @pl.loop(0, MODES)
    def _(m):
        @pl.when(mode_chip(m) != ctx)
        def _():
            end_copy(m, ctx).start()

        @pl.when(mode_chip(m) == ctx)
        def _():
            gath[lax.rem(m, per), ctx] = ends[m]

    def inside_step(t, state):
        x = x_at(t)
        state = tuple(state[m] * dec[m] + x for m in range(MODES))
        terms = [state[m] * wgt_ref[m] for m in range(MODES)]
        while len(terms) > 1:
            terms = [a + b for a, b in zip(terms[::2], terms[1::2])]
        ys[pl.ds(pl.multiple_of(t * 8, 8), 8), :] = terms[0]
        return state

    lax.fori_loop(0, BLK, inside_step, zeros, unroll=2)

    def reply_copy(mm, to, chip):
        return pltpu.make_async_remote_copy(
            reply.at[mm, to], enter.at[chip * per + mm], r_ss.at[mm, to], r_rs.at[chip * per + mm],
            device_id=(to, tp), device_id_type=MESH)

    @pl.when(core == 0)
    def _():
        chip = ctx // 2

        @pl.loop(0, nctx)
        def _(frm):
            @pl.when(frm != ctx)
            def _():
                for mm in range(per):
                    end_copy(chip * per + mm, frm).wait_recv()

        for mm in range(per):
            mode = chip * per + mm
            blkdec = blkdec_ref[mode]

            def block_step(p, carry):
                prefix[pl.ds(2 * p, 1), :] = carry[0]
                prefix[pl.ds(2 * p + 1, 1), :] = carry[1]
                code = row_of_ref[0, p]
                return tuple(
                    carry[g] * blkdec[g:g + 1] + gath[mm, code // 8, pl.ds(lax.rem(code, 8) + g, 1), :]
                    for g in range(2))

            start = (jnp.zeros((1, HD), F32), jnp.zeros((1, HD), F32))
            lax.fori_loop(0, nctx * NB, block_step, start, unroll=4)

            @pl.loop(0, nctx)
            def _(to):
                for b in range(NB):
                    pos = bo_ref[to * NB + b]
                    for g in range(2):
                        reply[mm, to, 2 * b + g:2 * b + g + 1] = prefix[pl.ds(2 * pos + g, 1), :]
                reply[mm, to, 2 * NB:8] = jnp.zeros((8 - 2 * NB, HD), F32)

                @pl.when(to != ctx)
                def _():
                    reply_copy(mm, to, chip).start()

                @pl.when(to == ctx)
                def _():
                    enter[chip * per + mm] = reply[mm, to]

    @pl.loop(0, half)
    def _(chip):
        @pl.when(2 * chip != ctx)
        def _():
            for mm in range(per):
                reply_copy(mm, ctx, chip).wait_recv()

    def carry_step(t, state):
        state = tuple(state[m] * dec[m] for m in range(MODES))
        terms = list(state)
        while len(terms) > 1:
            terms = [a + b for a, b in zip(terms[::2], terms[1::2])]
        rows = pl.ds(pl.multiple_of(t * 8, 8), 8)
        ys[rows, :] = ys[rows, :] + terms[0]
        return state

    lax.fori_loop(0, BLK, carry_step, tuple(enter[m] * wgt_ref[m] for m in range(MODES)), unroll=4)

    for b in range(NB):
        rows = slice(b * BLK, (b + 1) * BLK)
        for g in range(2):
            cols = slice(g * HD, (g + 1) * HD)
            conv = ys[pl.ds(2 * b + g, BLK, stride=8), :].astype(BF16).astype(F32)
            hout_ref[rows, cols] = (og_ref[rows, cols].astype(F32) * (
                conv + sg_ref[:, cols] * mixed[rows, cols].astype(F32))).astype(BF16)

    @pl.loop(0, ny)
    def _(j):
        for zz in range(2):
            sib_copy(j, zz).wait_send()

    @pl.loop(0, hs)
    def _(j):
        for zz in range(2):
            plus_copy(j, zz, 0).wait_send()
            minus_copy(j, zz, 1).wait_send()

            @pl.when(j < hs - 1)
            def _():
                plus_copy(j, zz, 1).wait_send()
                minus_copy(j, zz, 0).wait_send()

    for i in range(5):
        z_copy(i).wait_send()

    @pl.loop(1, ntp)
    def _(i):
        tp_copy(i, tp).wait_send()

    @pl.loop(0, MODES)
    def _(m):
        @pl.when(mode_chip(m) != ctx)
        def _():
            end_copy(m, ctx).wait_send()

    @pl.when(core == 0)
    def _():
        @pl.loop(0, nctx)
        def _(to):
            @pl.when(to != ctx)
            def _():
                for mm in range(per):
                    reply_copy(mm, to, ctx // 2).wait_send()


def per_device(nctx, ntp, queries, keys, values, out_gate, in_gate, norm_gain, skip_gain, rates, residues, block_order):
    ny = nctx // 4
    nblk = block_order.shape[0]
    per = max(1, MODES // (nctx // 2))
    vmem = pl.BlockSpec(memory_space=pltpu.VMEM)
    hbm = pl.BlockSpec(memory_space=pltpu.HBM)
    dma = pltpu.SemaphoreType.DMA
    return pl.pallas_call(
        functools.partial(body, nctx, ntp),
        out_shape=(jax.ShapeDtypeStruct((ROWS, 2 * HD), BF16), jax.ShapeDtypeStruct((ROWS, 2 * HD), BF16)),
        in_specs=[hbm] * 10,
        out_specs=(vmem, vmem),
        scratch_shapes=[
            pltpu.VMEM((ny, 2, 2, 2 * ROWS, HD), BF16),
            pltpu.VMEM((2, HD, ROWS), BF16),
            pltpu.VMEM((2 * ROWS, HD), BF16),
            pltpu.VMEM((HD, ROWS), BF16),
            pltpu.VMEM((2, HD + 16, ROWS), F32),
            pltpu.VMEM((2, 1, ROWS), F32),
            pltpu.VMEM((2, 1, ROWS), jnp.int32),
            pltpu.VMEM((ROWS, HD), BF16),
            pltpu.VMEM((ROWS, HD), BF16),
            pltpu.VMEM((1, ROWS), F32),
            pltpu.VMEM((1, ROWS), F32),
            pltpu.VMEM((ntp, 1, ROWS), F32),
            pltpu.VMEM((BLK * 8, HD), F32),
            pltpu.VMEM((BLK * 8, HD), F32),
            pltpu.VMEM((ROWS, 2 * HD), BF16),
            pltpu.VMEM((MODES, 8, HD), F32),
            pltpu.VMEM((per, nctx, 8, HD), F32),
            pltpu.VMEM((2 * nblk, HD), F32),
            pltpu.VMEM((per, nctx, 8, HD), F32),
            pltpu.VMEM((MODES, 8, HD), F32),
            *[pltpu.VMEM((ROWS, 2 * HD), BF16)] * 5, *[pltpu.VMEM((1, 2 * HD), F32)] * 2,
            *[pltpu.VMEM((MODES, 2 * HD), F32)] * 2, pltpu.SMEM((nblk,), jnp.int32),
            pltpu.VMEM((1, BLK), jnp.int32), pltpu.SMEM((1, BLK), jnp.int32),
            *[pltpu.VMEM((MODES, 8, HD), F32)] * 3, dma((10,)), dma((1,)),
            dma((ny // 2, 2, 2)), dma((ny // 2, 2, 2)), dma((ny // 2, 2, 2)), dma((ny // 2, 2, 2)),
            dma((ny, 2)), dma((ny, 2)), dma((5,)), dma((5,)),
            dma((ntp,)), dma((ntp,)), dma((MODES,)), dma((per, nctx)), dma((per, nctx)), dma((MODES,)),
        ],
        compiler_params=pltpu.CompilerParams(
            collective_id=0, has_side_effects=True, vmem_limit_bytes=62 * 1024 * 1024),
    )(block_order, queries, keys, values, out_gate, in_gate,
      norm_gain.reshape(1, -1), skip_gain.reshape(1, -1), rates.T, residues.T)


def solution(mesh):
    placed = (
        P("ctx", "tp"),
        P("ctx", "tp"),
        P("ctx", "tp"),
        P("ctx", "tp"),
        P("ctx", "tp"),
        P("tp"),
        P("tp"),
        P("tp", None),
        P("tp", None),
        P(),
    )
    return jax.shard_map(
        functools.partial(per_device, mesh.shape["ctx"], mesh.shape["tp"]),
        mesh=mesh,
        in_specs=placed,
        out_specs=(P("ctx", "tp"), P("ctx", "tp")),
        check_vma=False,
    )
```

```python
import functools
import math

import jax
import jax.numpy as jnp
from jax import lax
from jax.experimental import pallas as pl
from jax.experimental.pallas import tpu as pltpu
from jax.sharding import PartitionSpec as P

HD = 128
BLK = 128
MODES = 16
NB = 3
ROWS = NB * BLK
EXP_SCALE = math.log2(math.e) / math.sqrt(HD)
NEG = -1e30
MESH = pl.DeviceIdType.MESH
F32 = jnp.float32
BF16 = jnp.bfloat16


def body(
    nctx, ntp,
    bo_in,    q_in, k_in, v_in, og_in, ig_in, ng_in, sg_in, rates_in, residues_in,
    aout_ref, hout_ref,
    kv, qt, zsend_kv, zsend_q, acc, mx, qpos,
    oz_send, oz_recv, ss_send, ss_recv, sq, xs, ys, mixed,
    ends, gath, prefix, reply, enter,
    q_ref, k_ref, v_ref, og_ref, ig_ref, ng_ref, sg_ref, rates, residues, bo_ref, row_vec, row_of_ref,
    dec_ref, wgt_ref, blkdec_ref, in_sem, row_sem,
    plus_ss, plus_rs, minus_ss, minus_rs, sib_ss, sib_rs, z_ss, z_rs, tp_ss, tp_rs, e_ss, e_rs, r_ss, r_rs,
):
    ny = nctx // 4
    half = nctx // 2
    per = MODES // half if MODES >= half else 1
    ctx = lax.axis_index("ctx")
    tp = lax.axis_index("tp")
    core = lax.rem(ctx, 2)
    y = lax.rem(ctx // 2, ny)
    zh = ctx // half
    hs = ny // 2

    def at(z, yy, c):
        return z * half + lax.rem(yy + 2 * ny, ny) * 2 + c

    after = (at(zh, y + 1, core), tp)
    before = (at(zh, y - 1, core), tp)
    sib = (at(zh, y, 1 - core), tp)
    partner = (lax.rem(ctx + half, nctx), tp)

    loads = [
        pltpu.make_async_copy(src, dst, in_sem.at[i])
        for i, (src, dst) in enumerate((
            (v_in, v_ref), (k_in, k_ref), (q_in, q_ref), (bo_in, bo_ref), (rates_in, rates),
            (residues_in, residues), (ng_in, ng_ref), (sg_in, sg_ref), (ig_in, ig_ref), (og_in, og_ref)))]
    for load in loads:
        load.start()
    barrier = pltpu.get_barrier_semaphore()

    @pl.loop(1, nctx)
    def _(i):
        pl.semaphore_signal(barrier, inc=1, device_id=(lax.rem(ctx + i, nctx), tp), device_id_type=MESH)

    @pl.loop(1, ntp)
    def _(i):
        pl.semaphore_signal(barrier, inc=1, device_id=(ctx, lax.rem(tp + i, ntp)), device_id_type=MESH)

    own_cols = pl.ds(pl.multiple_of(zh * HD, HD), HD)
    oth_cols = pl.ds(pl.multiple_of((1 - zh) * HD, HD), HD)

    def put_kv(dst, cols):
        dst[0:ROWS, :] = k_ref[:, cols]
        for b in range(NB):
            blk = v_ref[b * BLK:(b + 1) * BLK, cols].astype(F32)
            dst[ROWS + b * BLK:ROWS + (b + 1) * BLK, :] = blk.T.astype(BF16)

    for load in loads[:3]:
        load.wait()
    put_kv(kv.at[0, 0, 0], own_cols)
    put_kv(zsend_kv, oth_cols)
    qt[0] = q_ref[:, own_cols].astype(F32).T.astype(BF16)
    zsend_q[...] = q_ref[:, oth_cols].astype(F32).T.astype(BF16)

    pl.semaphore_wait(barrier, nctx - 1 + ntp - 1)

    def plus_copy(j, zz, part):
        rows = pl.ds(part * ROWS, ROWS)
        return pltpu.make_async_remote_copy(
            kv.at[j, zz, 0, rows], kv.at[j + 1, zz, 0, rows],
            plus_ss.at[j, zz, part], plus_rs.at[j, zz, part],
            device_id=after, device_id_type=MESH)

    def minus_copy(j, zz, part):
        rows = pl.ds(part * ROWS, ROWS)
        return pltpu.make_async_remote_copy(
            kv.at[lax.rem(ny - j, ny), zz, 0, rows], kv.at[ny - 1 - j, zz, 0, rows],
            minus_ss.at[j, zz, part], minus_rs.at[j, zz, part],
            device_id=before, device_id_type=MESH)

    def launch(zz, part):
        if part == 0 or hs > 1:
            plus_copy(0, zz, part).start()
        if part == 1 or hs > 1:
            minus_copy(0, zz, part).start()

    def sib_copy(s, zz):
        return pltpu.make_async_remote_copy(
            kv.at[s, zz, 0], kv.at[s, zz, 1], sib_ss.at[s, zz], sib_rs.at[s, zz],
            device_id=sib, device_id_type=MESH)

    def z_copy(i):
        src, dst = ((zsend_kv.at[0:ROWS], kv.at[0, 1, 0, 0:ROWS]),
                    (zsend_kv.at[ROWS:2 * ROWS], kv.at[0, 1, 0, ROWS:2 * ROWS]),
                    (zsend_q, qt.at[1]),
                    (ss_send, ss_recv),
                    (oz_send, oz_recv))[i]
        return pltpu.make_async_remote_copy(
            src, dst, z_ss.at[i], z_rs.at[i], device_id=partner, device_id_type=MESH)

    launch(0, 0)
    z_copy(2).start()
    launch(0, 1)
    sib_copy(0, 0).start()
    z_copy(0).start()
    z_copy(1).start()

    for load in loads[3:6]:
        load.wait()
    lane = lax.broadcasted_iota(jnp.int32, (1, ROWS), 1)
    for zz in range(2):
        dev = at(jnp.where(zz == 0, zh, 1 - zh), y, core)
        p0 = bo_ref[dev * NB]
        p1 = bo_ref[dev * NB + 1]
        p2 = bo_ref[dev * NB + 2]
        qpos[zz] = jnp.where(lane < BLK, p0, jnp.where(lane < 2 * BLK, p1, p2))
    mx[...] = jnp.full(mx.shape, NEG, F32)
    acc[...] = jnp.zeros(acc.shape, F32)
    ones = jnp.ones((16, 2 * ROWS), BF16)

    def unit(j, zk, zqs=(0, 1)):
        qtv = jnp.concatenate([qt[zq] for zq in zqs], axis=1)
        qv = jnp.concatenate([qpos[zq] for zq in zqs], axis=1)
        m_old = jnp.concatenate([mx[zq] for zq in zqs], axis=1)
        zsrc = zh if zk == 0 else 1 - zh
        srcs = (at(zsrc, y - j, core), at(zsrc, y - j, 1 - core))
        tiles = []
        m_new = m_old
        for d in range(2):
            st = jnp.dot(kv[j, zk, d, 0:ROWS], qtv, preferred_element_type=F32)
            for b in range(NB):
                tile = st[b * BLK:(b + 1) * BLK]
                if d == 0 and zk in zqs:
                    rel = (lax.broadcasted_iota(jnp.int32, (BLK, BLK), 0)
                           - lax.broadcasted_iota(jnp.int32, (BLK, BLK), 1))
                    limit = jnp.where(j == 0, 0, BLK)
                    spot = zqs.index(zk) * NB + b
                    parts = [tile[:, i * BLK:(i + 1) * BLK] for i in range(NB * len(zqs))]
                    parts[spot] = jnp.where(rel <= limit, parts[spot], -jnp.inf)
                    tile = jnp.concatenate(parts, axis=1)
                vis = bo_ref[srcs[d] * NB + b] <= qv
                m_new = jnp.maximum(m_new, jnp.where(vis, jnp.max(tile, axis=0, keepdims=True), NEG))
                tiles.append((tile, vis))
        mc = m_new * EXP_SCALE
        probs = [
            jnp.exp2(tile * EXP_SCALE - jnp.where(vis, mc, jnp.inf)).astype(BF16) for tile, vis in tiles]
        vts = [
            kv[j, zk, d, ROWS + b * BLK:ROWS + (b + 1) * BLK] for d in range(2) for b in range(NB)]
        vt = jnp.concatenate([jnp.concatenate(vts, axis=1), ones], axis=0)
        summed = jnp.dot(vt, jnp.concatenate(probs, axis=0), preferred_element_type=F32)
        scale = jnp.exp2(m_old * EXP_SCALE - mc)
        for i, zq in enumerate(zqs):
            cols = slice(i * ROWS, (i + 1) * ROWS)
            acc[zq] = acc[zq] * scale[:, cols] + summed[:, cols]
            mx[zq] = m_new[:, cols]

    def take(t, zz, part):
        far = hs + 1 if part == 0 else hs
        near = hs + 1 if part == 1 else hs

        @pl.when(t < far)
        def _():
            plus_copy(t - 1, zz, part).wait_recv()

            @pl.when(t + 1 < far)
            def _():
                plus_copy(t, zz, part).start()

        @pl.when(t < near)
        def _():
            minus_copy(t - 1, zz, part).wait_recv()

            @pl.when(t + 1 < near)
            def _():
                minus_copy(t, zz, part).start()

        if part == 1:
            sib_copy(t, zz).start()

            @pl.when(t < hs)
            def _():
                sib_copy(ny - t, zz).start()

    take(1, 0, 0)
    nblk = nctx * NB
    spot = lax.broadcasted_iota(jnp.int32, (1, BLK), 1)

    def place(i, codes):
        code = lax.div(i, NB) * 8 + lax.rem(i, NB) * 2
        return jnp.where(spot == bo_ref[i], code, codes)

    row_vec[...] = lax.fori_loop(0, nblk, place, jnp.zeros((1, BLK), jnp.int32), unroll=4)
    row_copy = pltpu.make_async_copy(row_vec, row_of_ref, row_sem.at[0])
    row_copy.start()
    take(1, 0, 1)
    even = lax.rem(lax.broadcasted_iota(jnp.int32, (8, HD), 0), 2) == 0

    @pl.loop(0, MODES)
    def _(m):
        def pair(ref):
            row = ref[pl.ds(m, 1), :]
            return jnp.where(even, row[:, 0:HD], row[:, HD:2 * HD])

        rate = pair(rates)
        two = 2.0 * rate
        series = 1.0 - two * (1 / 6)
        for k in (5, 4, 3, 2):
            series = 1.0 - two * series * (1 / k)
        dec_ref[m] = jnp.exp(-rate)
        blkdec_ref[m] = jnp.exp(-BLK * rate)
        wgt_ref[m] = pair(residues) * jnp.sqrt(two * series)

    row_copy.wait()
    z_copy(2).wait_recv()

    def attend(j, zz):
        sib_copy(j, zz).wait_recv()
        unit(j, zz)

    def launch_far():
        z_copy(0).wait_recv()
        launch(1, 0)
        z_copy(1).wait_recv()
        launch(1, 1)
        sib_copy(0, 1).start()

    def lead(zz, first, last, shift):
        @pl.loop(first, last)
        def _(s):
            take(s + shift, zz, 0)
            attend(s, zz)
            take(s + shift, zz, 1)

            @pl.when(s > 0)
            def _():
                attend(ny - s, zz)

    def rest(zz, first, last):
        @pl.loop(first, last)
        def _(j):
            attend(j, zz)

    if hs > 2:
        lead(0, 0, hs - 2, 2)
        launch_far()
        rest(0, hs - 2, hs - 1)
        take(hs, 0, 0)
        take(hs, 0, 1)
        rest(0, hs + 2, hs + 3)
        take(1, 1, 0)
        take(1, 1, 1)
        rest(0, hs - 1, hs + 2)
        rest(1, 0, 1)
        lead(1, 1, hs, 1)
    else:
        lead(0, 0, hs - 1, 2)
        launch_far()
        rest(0, hs - 1, min(hs + 2, ny))
        lead(1, 0, hs, 1)

    sib_copy(hs, 1).wait_recv()
    unit(hs, 1, (1,))

    def finish(zq):
        whole = acc[zq]
        out = (whole[0:HD] / whole[HD:HD + 1]).astype(BF16).astype(F32)
        return jnp.sum(out * out, axis=0, keepdims=True), out.T.astype(BF16)

    squares, out = finish(1)
    ss_send[...] = squares
    oz_send[...] = out
    z_copy(3).start()
    z_copy(4).start()
    unit(hs, 1, (0,))
    squares, out = finish(0)
    aout_ref[:, own_cols] = out
    z_copy(3).wait_recv()
    sq[pl.ds(tp, 1)] = (squares + ss_recv[...])[None]

    def tp_copy(i, frm):
        return pltpu.make_async_remote_copy(
            sq.at[frm], sq.at[frm], tp_ss.at[i], tp_rs.at[frm],
            device_id=(ctx, lax.rem(tp + i, ntp)), device_id_type=MESH)

    @pl.loop(1, ntp)
    def _(i):
        tp_copy(i, tp).start()

    z_copy(4).wait_recv()
    aout_ref[:, oth_cols] = oz_recv[...]

    @pl.loop(1, ntp)
    def _(i):
        tp_copy(i, lax.rem(tp + i, ntp)).wait_recv()

    for load in loads[6:]:
        load.wait()
    square_sum = jnp.sum(sq[...], axis=0)
    scaled = lax.rsqrt(square_sum / (ntp * 2 * HD) + 1e-06)
    scaled = jnp.broadcast_to(scaled, (BLK, ROWS)).T
    for b in range(NB):
        rows = slice(b * BLK, (b + 1) * BLK)
        for g in range(2):
            cols = slice(g * HD, (g + 1) * HD)
            val = (aout_ref[rows, cols].astype(F32) * scaled[rows] * ng_ref[:, cols]
                   * ig_ref[rows, cols].astype(F32)).astype(BF16)
            mixed[rows, cols] = val
            xs[pl.ds(2 * b + g, BLK, stride=8), :] = val.astype(F32)
    for r in (2 * NB, 2 * NB + 1):
        xs[pl.ds(r, BLK, stride=8), :] = jnp.zeros((BLK, HD), F32)

    def x_at(t):
        return xs[pl.ds(pl.multiple_of(t * 8, 8), 8), :]

    dec = [dec_ref[m] for m in range(MODES)]
    zeros = tuple(jnp.zeros((8, HD), F32) for _ in range(MODES))

    def end_step(t, state):
        x = x_at(t)
        return tuple(state[m] * dec[m] + x for m in range(MODES))

    state = lax.fori_loop(0, BLK, end_step, zeros, unroll=4)
    for m in range(MODES):
        ends[m] = state[m]

    def mode_chip(m):
        return 2 * (m // per)

    def end_copy(m, frm):
        return pltpu.make_async_remote_copy(
            ends.at[m], gath.at[lax.rem(m, per), frm], e_ss.at[m], e_rs.at[lax.rem(m, per), frm],
            device_id=(mode_chip(m), tp), device_id_type=MESH)

    @pl.loop(0, MODES)
    def _(m):
        @pl.when(mode_chip(m) != ctx)
        def _():
            end_copy(m, ctx).start()

        @pl.when(mode_chip(m) == ctx)
        def _():
            gath[lax.rem(m, per), ctx] = ends[m]

    def inside_step(t, state):
        x = x_at(t)
        state = tuple(state[m] * dec[m] + x for m in range(MODES))
        terms = [state[m] * wgt_ref[m] for m in range(MODES)]
        while len(terms) > 1:
            terms = [a + b for a, b in zip(terms[::2], terms[1::2])]
        ys[pl.ds(pl.multiple_of(t * 8, 8), 8), :] = terms[0]
        return state

    lax.fori_loop(0, BLK, inside_step, zeros, unroll=2)

    def reply_copy(mm, to, chip):
        return pltpu.make_async_remote_copy(
            reply.at[mm, to], enter.at[chip * per + mm], r_ss.at[mm, to], r_rs.at[chip * per + mm],
            device_id=(to, tp), device_id_type=MESH)

    @pl.when(core == 0)
    def _():
        chip = ctx // 2

        @pl.loop(0, nctx)
        def _(frm):
            @pl.when(frm != ctx)
            def _():
                for mm in range(per):
                    end_copy(chip * per + mm, frm).wait_recv()

        for mm in range(per):
            mode = chip * per + mm
            blkdec = blkdec_ref[mode]

            def block_step(p, carry):
                prefix[pl.ds(2 * p, 1), :] = carry[0]
                prefix[pl.ds(2 * p + 1, 1), :] = carry[1]
                code = row_of_ref[0, p]
                return tuple(
                    carry[g] * blkdec[g:g + 1] + gath[mm, code // 8, pl.ds(lax.rem(code, 8) + g, 1), :]
                    for g in range(2))

            start = (jnp.zeros((1, HD), F32), jnp.zeros((1, HD), F32))
            lax.fori_loop(0, nctx * NB, block_step, start, unroll=8)

            @pl.loop(0, nctx)
            def _(to):
                for b in range(NB):
                    pos = bo_ref[to * NB + b]
                    for g in range(2):
                        reply[mm, to, 2 * b + g:2 * b + g + 1] = prefix[pl.ds(2 * pos + g, 1), :]
                reply[mm, to, 2 * NB:8] = jnp.zeros((8 - 2 * NB, HD), F32)

                @pl.when(to != ctx)
                def _():
                    reply_copy(mm, to, chip).start()

                @pl.when(to == ctx)
                def _():
                    enter[chip * per + mm] = reply[mm, to]

    @pl.loop(0, half)
    def _(chip):
        @pl.when(2 * chip != ctx)
        def _():
            for mm in range(per):
                reply_copy(mm, ctx, chip).wait_recv()

    def carry_step(t, state):
        state = tuple(state[m] * dec[m] for m in range(MODES))
        terms = list(state)
        while len(terms) > 1:
            terms = [a + b for a, b in zip(terms[::2], terms[1::2])]
        rows = pl.ds(pl.multiple_of(t * 8, 8), 8)
        ys[rows, :] = ys[rows, :] + terms[0]
        return state

    lax.fori_loop(0, BLK, carry_step, tuple(enter[m] * wgt_ref[m] for m in range(MODES)), unroll=4)

    for b in range(NB):
        rows = slice(b * BLK, (b + 1) * BLK)
        for g in range(2):
            cols = slice(g * HD, (g + 1) * HD)
            conv = ys[pl.ds(2 * b + g, BLK, stride=8), :].astype(BF16).astype(F32)
            hout_ref[rows, cols] = (og_ref[rows, cols].astype(F32) * (
                conv + sg_ref[:, cols] * mixed[rows, cols].astype(F32))).astype(BF16)

    @pl.loop(0, ny)
    def _(j):
        for zz in range(2):
            sib_copy(j, zz).wait_send()

    @pl.loop(0, hs)
    def _(j):
        for zz in range(2):
            plus_copy(j, zz, 0).wait_send()
            minus_copy(j, zz, 1).wait_send()

            @pl.when(j < hs - 1)
            def _():
                plus_copy(j, zz, 1).wait_send()
                minus_copy(j, zz, 0).wait_send()

    for i in range(5):
        z_copy(i).wait_send()

    @pl.loop(1, ntp)
    def _(i):
        tp_copy(i, tp).wait_send()

    @pl.loop(0, MODES)
    def _(m):
        @pl.when(mode_chip(m) != ctx)
        def _():
            end_copy(m, ctx).wait_send()

    @pl.when(core == 0)
    def _():
        @pl.loop(0, nctx)
        def _(to):
            @pl.when(to != ctx)
            def _():
                for mm in range(per):
                    reply_copy(mm, to, ctx // 2).wait_send()


def per_device(nctx, ntp, queries, keys, values, out_gate, in_gate, norm_gain, skip_gain, rates, residues, block_order):
    ny = nctx // 4
    nblk = block_order.shape[0]
    per = max(1, MODES // (nctx // 2))
    vmem = pl.BlockSpec(memory_space=pltpu.VMEM)
    hbm = pl.BlockSpec(memory_space=pltpu.HBM)
    dma = pltpu.SemaphoreType.DMA
    return pl.pallas_call(
        functools.partial(body, nctx, ntp),
        out_shape=(jax.ShapeDtypeStruct((ROWS, 2 * HD), BF16), jax.ShapeDtypeStruct((ROWS, 2 * HD), BF16)),
        in_specs=[hbm] * 10,
        out_specs=(vmem, vmem),
        scratch_shapes=[
            pltpu.VMEM((ny, 2, 2, 2 * ROWS, HD), BF16),
            pltpu.VMEM((2, HD, ROWS), BF16),
            pltpu.VMEM((2 * ROWS, HD), BF16),
            pltpu.VMEM((HD, ROWS), BF16),
            pltpu.VMEM((2, HD + 16, ROWS), F32),
            pltpu.VMEM((2, 1, ROWS), F32),
            pltpu.VMEM((2, 1, ROWS), jnp.int32),
            pltpu.VMEM((ROWS, HD), BF16),
            pltpu.VMEM((ROWS, HD), BF16),
            pltpu.VMEM((1, ROWS), F32),
            pltpu.VMEM((1, ROWS), F32),
            pltpu.VMEM((ntp, 1, ROWS), F32),
            pltpu.VMEM((BLK * 8, HD), F32),
            pltpu.VMEM((BLK * 8, HD), F32),
            pltpu.VMEM((ROWS, 2 * HD), BF16),
            pltpu.VMEM((MODES, 8, HD), F32),
            pltpu.VMEM((per, nctx, 8, HD), F32),
            pltpu.VMEM((2 * nblk, HD), F32),
            pltpu.VMEM((per, nctx, 8, HD), F32),
            pltpu.VMEM((MODES, 8, HD), F32),
            *[pltpu.VMEM((ROWS, 2 * HD), BF16)] * 5, *[pltpu.VMEM((1, 2 * HD), F32)] * 2,
            *[pltpu.VMEM((MODES, 2 * HD), F32)] * 2, pltpu.SMEM((nblk,), jnp.int32),
            pltpu.VMEM((1, BLK), jnp.int32), pltpu.SMEM((1, BLK), jnp.int32),
            *[pltpu.VMEM((MODES, 8, HD), F32)] * 3, dma((10,)), dma((1,)),
            dma((ny // 2, 2, 2)), dma((ny // 2, 2, 2)), dma((ny // 2, 2, 2)), dma((ny // 2, 2, 2)),
            dma((ny, 2)), dma((ny, 2)), dma((5,)), dma((5,)),
            dma((ntp,)), dma((ntp,)), dma((MODES,)), dma((per, nctx)), dma((per, nctx)), dma((MODES,)),
        ],
        compiler_params=pltpu.CompilerParams(
            collective_id=0, has_side_effects=True, vmem_limit_bytes=62 * 1024 * 1024),
    )(block_order, queries, keys, values, out_gate, in_gate,
      norm_gain.reshape(1, -1), skip_gain.reshape(1, -1), rates.T, residues.T)


def solution(mesh):
    placed = (
        P("ctx", "tp"),
        P("ctx", "tp"),
        P("ctx", "tp"),
        P("ctx", "tp"),
        P("ctx", "tp"),
        P("tp"),
        P("tp"),
        P("tp", None),
        P("tp", None),
        P(),
    )
    return jax.shard_map(
        functools.partial(per_device, mesh.shape["ctx"], mesh.shape["tp"]),
        mesh=mesh,
        in_specs=placed,
        out_specs=(P("ctx", "tp"), P("ctx", "tp")),
        check_vma=False,
    )
```
